32 devices in a mesh: row: 4 (over z), rhs: 8 (over y, x, core).
Axes of the slice: x: 2, y: 2, z: 4, core: 2. Of those that a mesh axis runs over, the one named last changes fastest.
Arguments:
- rhs_blocks: bfloat16 [8, 4, 512, 16384], P(None, 'row', None, 'rhs'), may hold values from -6 to 6
- panel: bfloat16 [8, 4, 512, 1536], P(None, 'row', 'rhs'), may hold values from -0.1875 to 0.1875
- inverse_diag: bfloat16 [3, 512, 512], replicated, may hold values from -0.25 to 0.25
Outputs:
- updated: bfloat16 [8, 4, 512, 16384], P(None, 'row', None, 'rhs')
The draws below stay inside these ranges and needn't reach their ends.
All inputs are finite; a program needn't handle non-finite values.
Results may differ from the reference program's by a relative error of at most 0.0056.
Values may be sent and summed in bfloat16 or wider, within the bound.
No kernel may reach another device: no remote copies, remote signals or barrier semaphores. Data moves between devices by JAX's collectives and lax.ppermute only.
A program may use at most 128 MiB of HBM per device.

```python
import jax
import jax.numpy as jnp

BS = 512
NRHS = 16384
KB = 3
CYC = 8
N_ROW = 4


def shard_levels(stream_key, dims, shards, low, largest):
    gain, own = 1.0, jax.random.fold_in(stream_key, 6)
    for dim, blocks in shards:
        heights = jnp.exp(jax.random.uniform(jax.random.fold_in(own, dim), (blocks,), jnp.float32, low / len(shards), largest / len(shards)))
        gain = gain * jnp.repeat(heights, dims[dim] // blocks).reshape([-1 if axis == dim else 1 for axis in range(len(dims))])
    return gain


def scatter_about(key, extent, spread, reach, pieces=(), held_as=jnp.bfloat16):
    array = spread * jax.random.normal(key, extent, jnp.float32)
    if pieces:
        array = array * shard_levels(key, extent, pieces, -0.22, 0.18)
    return jnp.clip(array, -reach, reach).astype(held_as)


def setup_inputs(seed: int = 0) -> dict:
    arg_keys = jax.random.split(jax.random.key(seed), 4)
    return {
        "rhs_blocks": scatter_about(arg_keys[0], (CYC, N_ROW, BS, NRHS), 1.0, 6.0, ((1, 4), (3, 8))),
        "panel": scatter_about(arg_keys[1], (CYC, N_ROW, BS, KB * BS), (2 * BS) ** -0.5, 0.1875, ((1, 4), (2, 8))),
        "inverse_diag": scatter_about(arg_keys[2], (KB, BS, BS), BS ** -0.5, 0.25),
    }


def reference(rhs_blocks, panel, inverse_diag):
    total = CYC * N_ROW
    flat_rhs = rhs_blocks.reshape(total, BS, NRHS)
    flat_panel = panel.reshape(total, BS, KB * BS)
    work = [flat_rhs[index].astype(jnp.float32) for index in range(total)]
    solved = []
    for block_step in range(KB):
        answer = jnp.dot(inverse_diag[block_step], work[block_step].astype(jnp.bfloat16), preferred_element_type=jnp.float32).astype(jnp.bfloat16)
        solved.append(answer)
        for index in range(block_step + 1, total):
            factor = flat_panel[index, :, block_step * BS:(block_step + 1) * BS]
            work[index] = work[index] - jnp.dot(factor, answer, preferred_element_type=jnp.float32)
    result = [solved[index] if index < KB else work[index].astype(jnp.bfloat16) for index in range(total)]
    return jnp.stack(result).reshape(CYC, N_ROW, BS, NRHS)
```

```python
import functools

import jax
import jax.numpy as jnp
from jax import lax
from jax.experimental import pallas as pl
from jax.experimental.pallas import tpu as pltpu
from jax.sharding import PartitionSpec as P

LANES = 128
TILE = 512


def halving(total):
    parts, start = [], 0
    smallest = max(total // 8, LANES)
    while total - start > smallest:
        width = (total - start) // 2
        parts.append((start, width))
        start += width
    parts.append((start, total - start))
    return parts


def chunk_kernel(cfg, *refs):
    refs = list(refs)
    scal, rhs, inv = refs[:3]
    rest = refs[3:]
    shifts_r = rest[: cfg["n_r"]]
    rest = rest[cfg["n_r"] :]
    shifts_l = rest[: cfg["n_l"]]
    rest = rest[cfg["n_l"] :]
    pieces = rest[: cfg["n_p"]]
    rest = rest[cfg["n_p"] :]
    couplings = rest[: cfg["n_c"]]
    rest = rest[cfg["n_c"] :]
    if cfg["aliased"]:
        rest = rest[1:]
    out, blocks, solved, inv_s, coup_s, panel_s, rows_s, sem_b, sem_i, sem_c, sem_p, sem_r, sem_o = rest
    rank, me = scal[0], scal[1]
    kb, size, col, width = cfg["kb"], cfg["size"], cfg["col"], cfg["width"]
    slots = cfg["slots"]
    sub = size // slots

    def copy(src, dst, sem):
        pltpu.make_async_copy(src, dst, sem).start()

    def landed(dst, sem):
        pltpu.make_async_copy(dst, dst, sem).wait()

    copy(inv, inv_s, sem_i)
    for b in range(kb):
        for r in range(cfg["rows"]):
            if r == b:
                src = rhs.at[0, 0, :, pl.ds(col, width)]
            elif r > b:
                src = shifts_r[r - b - 1].at[:, pl.ds(cfg["off_r"], width)]
            else:
                src = shifts_l[b - r - 1].at[:, pl.ds(cfg["off_l"], width)]

            @pl.when(rank == r)
            def _(src=src, b=b):
                copy(src, blocks.at[b], sem_b.at[b])

    for ref, masks in zip(couplings, cfg["coup_masks"]):
        for at, m in enumerate(masks):
            copy(ref.at[at], coup_s.at[me ^ m], sem_c)
    for ref, (m, start, count) in zip(pieces, cfg["where"]):
        copy(ref, panel_s.at[m, pl.ds(start, count)], sem_p.at[m])
    for m in range(slots):
        copy(
            rhs.at[:, 0, pl.ds((me ^ m) * sub, sub), pl.ds(col, width)],
            rows_s.at[m],
            sem_r.at[m],
        )

    landed(inv_s, sem_i)
    for k in range(kb):
        landed(blocks.at[k], sem_b.at[k])
        if k == 0:
            now = blocks[0]
        else:
            if k == 1:
                landed(coup_s, sem_c)
            base = size * (k * (k - 1) // 2)
            link = coup_s[:, :, base : base + size * k].reshape(size, size * k)
            known = solved[: k * slots].reshape(size * k, width)
            now = blocks[k].astype(jnp.float32) - jnp.dot(
                link, known, preferred_element_type=jnp.float32
            )
            now = now.astype(jnp.bfloat16)
        answer = jnp.dot(inv_s[k], now, preferred_element_type=jnp.float32)
        solved[k * slots : (k + 1) * slots] = answer.astype(jnp.bfloat16).reshape(slots, sub, width)

    cycles = rows_s.shape[1]

    def step(m, carry):
        landed(panel_s.at[m], sem_p.at[m])
        landed(rows_s.at[m], sem_r.at[m])
        change = jnp.dot(
            panel_s[m].reshape(cycles * sub, kb * size),
            solved[...].reshape(kb * size, width),
            preferred_element_type=jnp.float32,
        )
        new = rows_s[m].astype(jnp.float32) - change.reshape(cycles, sub, width)
        rows_s[m] = new.astype(jnp.bfloat16)

        @pl.when(rank < kb)
        def _():
            rows_s[m, 0] = solved[rank * slots + (me ^ m)]

        copy(
            rows_s.at[m],
            out.at[:, 0, pl.ds((me ^ m) * sub, sub), pl.ds(col, width)],
            sem_o.at[m],
        )
        return carry

    lax.fori_loop(0, slots, step, 0)
    for m in range(slots):
        landed(rows_s.at[m], sem_o.at[m])


def run_chunk(cfg, scal, rhs, inv, shifts_r, shifts_l, pieces, couplings, out):
    kb, size, width, slots = cfg["kb"], cfg["size"], cfg["width"], cfg["slots"]
    cycles = rhs.shape[0]
    sub = size // slots
    operands = [scal, rhs, inv, *shifts_r, *shifts_l, *pieces, *couplings]
    cfg = dict(
        cfg,
        n_r=len(shifts_r),
        n_l=len(shifts_l),
        n_p=len(pieces),
        n_c=len(couplings),
        aliased=out is not None,
    )
    aliases = {}
    if out is not None:
        aliases = {len(operands): 0}
        operands.append(out)
    any_spec = pl.BlockSpec(memory_space=pl.ANY)
    specs = [pl.BlockSpec(memory_space=pltpu.SMEM)] + [any_spec] * (len(operands) - 1)
    bf16 = jnp.bfloat16
    return pl.pallas_call(
        functools.partial(chunk_kernel, cfg),
        out_shape=jax.ShapeDtypeStruct(rhs.shape, rhs.dtype),
        in_specs=specs,
        out_specs=any_spec,
        scratch_shapes=[
            pltpu.VMEM((kb, size, width), bf16),
            pltpu.VMEM((kb * slots, sub, width), bf16),
            pltpu.VMEM((kb, size, size), bf16),
            pltpu.VMEM((slots, sub, size * kb * (kb - 1) // 2), bf16),
            pltpu.VMEM((slots, cycles, sub, kb * size), bf16),
            pltpu.VMEM((slots, cycles, sub, width), bf16),
            pltpu.SemaphoreType.DMA((kb,)),
            pltpu.SemaphoreType.DMA,
            pltpu.SemaphoreType.DMA,
            pltpu.SemaphoreType.DMA((slots,)),
            pltpu.SemaphoreType.DMA((slots,)),
            pltpu.SemaphoreType.DMA((slots,)),
        ],
        input_output_aliases=aliases,
        compiler_params=pltpu.CompilerParams(vmem_limit_bytes=48 << 20),
        cost_estimate=pl.CostEstimate(
            flops=2 * size * kb * size * width * (cycles + 2),
            bytes_accessed=2 * (slots * cycles * sub * kb * size + 2 * cycles * size * width),
            transcendentals=0,
        ),
        name="chunk_%d" % cfg["col"],
    )(*operands)


def per_device(rhs_blocks, panel, inverse_diag):
    row_rank = lax.axis_index("row")
    rows = lax.axis_size("row")
    me = lax.axis_index("rhs")
    slots = lax.axis_size("rhs")
    cycles = rhs_blocks.shape[0]
    columns = rhs_blocks.shape[3]
    kb, size = inverse_diag.shape[0], inverse_diag.shape[1]
    assert rows >= kb and slots & (slots - 1) == 0 and slots >= 2
    scal = jnp.stack([row_rank, me]).astype(jnp.int32)
    panel = panel[:, 0]
    own = rhs_blocks[0, 0]

    def swap(x, mask):
        return lax.ppermute(x, "rhs", [(i, i ^ mask) for i in range(slots)])

    piece = panel[0, :, : (kb - 1) * size]
    todo = [(b, r) for b in range(1, kb) for r in range(rows) if r != b]
    todo.sort(key=lambda t: abs(t[0] - t[1]))
    packs = []
    for b, r in todo:
        for pack in packs:
            if all(b != s and r != d for s, d in pack):
                pack.append((b, r))
                break
        else:
            packs.append([(b, r)])
    got = [lax.ppermute(piece, "row", pack) for pack in packs]
    parts = []
    for b in range(1, kb):
        mine = piece[:, : b * size]
        for pack, array in zip(packs, got):
            for s, d in pack:
                if s == b:
                    mine = jnp.where(row_rank == d, array[:, : b * size], mine)
        parts.append(mine)
    coup = jnp.concatenate(parts, axis=1)[None]
    masks = [0]
    bit = 2
    while bit < slots:
        coup = jnp.concatenate([coup, swap(coup, bit)], axis=0)
        masks += [m ^ bit for m in masks]
        bit *= 2
    couplings = [coup, swap(coup, 1)]
    coup_masks = [masks, [m ^ 1 for m in masks]]

    held = {0: [(panel, 0)]}
    if slots == 8:
        half = cycles // 2
        held[2] = [(swap(panel, 2), 0)]
        held[4] = [(swap(panel, 4), 0)]
        held[6] = [
            (swap(held[2][0][0][:half], 4), 0),
            (swap(held[4][0][0][half:], 2), half),
        ]
    else:
        for m in range(2, slots, 2):
            held[m] = [(swap(panel, m), 0)]
    for m in list(held):
        held[m ^ 1] = [(swap(x, 1), at) for x, at in held[m]]
    pieces, where = [], []
    for m in sorted(held):
        for x, at in held[m]:
            pieces.append(x)
            where.append((m, at, x.shape[0]))

    def line(x, step, sign):
        pairs = []
        for r in range(rows):
            to, b = r + sign, r - sign * (step - 1)
            if 0 <= b < kb and 0 <= to < rows:
                pairs.append((r, to))
        return lax.ppermute(x, "row", pairs)

    chunks = halving(columns)
    first = chunks[0][1]
    left = []
    for at, width in [(0, first), (first, columns - first)]:
        x, steps = own[:, at : at + width], []
        for step in range(1, kb):
            x = line(x, step, -1)
            steps.append(x)
        left.append((at, steps))
    out = None
    for index, (start, width) in enumerate(chunks):
        x, steps = own[:, start : start + width], []
        for step in range(1, rows):
            x = line(x, step, 1)
            steps.append(x)
        l_at, l_steps = left[0] if index == 0 else left[1]
        tile = min(width, TILE)
        for off in range(0, width, tile):
            cfg = dict(
                kb=kb,
                size=size,
                rows=rows,
                slots=slots,
                col=start + off,
                width=tile,
                off_r=off,
                off_l=start + off - l_at,
                where=where,
                coup_masks=coup_masks,
            )
            out = run_chunk(
                cfg, scal, rhs_blocks, inverse_diag, steps, l_steps, pieces, couplings, out
            )
    return out


def solution(mesh):
    in_specs = (P(None, "row", None, "rhs"), P(None, "row", "rhs", None), P())
    out_specs = P(None, "row", None, "rhs")
    return jax.shard_map(
        per_device, mesh=mesh, in_specs=in_specs, out_specs=out_specs, check_vma=False
    )
```
